32 devices in a mesh: blk: 4 (over y, x), head: 4 (over z), grp: 2 (over core).
Axes of the slice: x: 2, y: 2, z: 4, core: 2. Of those that a mesh axis runs over, the one named last changes fastest.
Arguments:
- t_query: bfloat16 [4096, 4096], P('blk', ('head', 'grp')), may hold values from -80 to 80
- t_key: bfloat16 [4096, 4096], P('blk', ('head', 'grp')), may hold values from -80 to 80
- t_value: bfloat16 [4096, 4096], P('blk', ('head', 'grp')), may hold values from -6 to 6
- t_out: bfloat16 [4096, 4096], P(('head', 'grp')), may hold values from -0.09375 to 0.09375
- s_query: bfloat16 [4096, 2048], P('blk', ('head', 'grp')), may hold values from -80 to 80
- s_key: bfloat16 [4096, 2048], P('blk', ('head', 'grp')), may hold values from -80 to 80
- s_value: bfloat16 [4096, 2048], P('blk', ('head', 'grp')), may hold values from -6 to 6
- s_out: bfloat16 [2048, 4096], P(('head', 'grp')), may hold values from -0.125 to 0.125
- segments: int32 [4096], P('blk'), may hold values from 0 to 1, never falling along the last dimension, each value on 1 to 4032 neighbouring positions
- selection: int32 [64, 16], P('blk'), may hold values from 0 to 63, as said below
Outputs:
- mismatch: float32 [4096, 4096], P('blk', ('head', 'grp'))
- s_dq: float32 [4096, 2048], P('blk', ('head', 'grp'))
- s_dk: float32 [4096, 2048], P('blk', ('head', 'grp'))
- s_dv: float32 [4096, 2048], P('blk', ('head', 'grp'))
The draws below stay inside these ranges and needn't reach their ends.
Inputs may be any that keep to these rules, and one draw needn't show every extreme that they name: `selection`: entry 0 of row b is b itself; for b >= 32, entry 1 of row b is b - 32; every entry of row b lies between 0 and b; entries of a row may repeat. `segments`: document numbers never fall along the sequence.
All inputs are finite; a program needn't handle non-finite values.
Results may differ from the reference program's by a relative error of at most 0.015.
Values may be sent and summed in bfloat16 or wider, within the bound.
A program may use at most 128 MiB of HBM per device.

```python
import math
import jax
import jax.numpy as jnp
import numpy as np
from jax import lax

D = 4096
TH = 32
SH = 16
HD = 128
BS = 64
NSEL = 16
TOKENS = 4096
N_HEAD = 4
N_GRP = 2


def drawn_pair(key, columns, salt):
    folded = jax.random.fold_in(key, salt)
    key_rows = jax.random.normal(jax.random.fold_in(folded, 1), (TOKENS, columns), jnp.float32)
    queries = 2.5 * jax.random.normal(jax.random.fold_in(folded, 2), (TOKENS, columns), jnp.float32)
    return (queries.astype(jnp.bfloat16), key_rows.astype(jnp.bfloat16))


def draw_t_query(key, part):
    return drawn_pair(key, TH * HD, 101)[0]


def draw_t_key(key, part):
    return drawn_pair(key, TH * HD, 101)[1]


def draw_s_query(key, part):
    return drawn_pair(key, SH * HD, 202)[0]


def draw_s_key(key, part):
    return drawn_pair(key, SH * HD, 202)[1]


def draw_selection(key, part):
    block_count = TOKENS // BS
    rows = jnp.arange(block_count, dtype=jnp.int32)
    upper_bound = rows[:, None] + 1
    first_back = jax.random.randint(jax.random.fold_in(key, 303), (block_count, NSEL), 0, upper_bound, dtype=jnp.int32)
    second_back = jax.random.randint(jax.random.fold_in(key, 304), (block_count, NSEL), 0, upper_bound, dtype=jnp.int32)
    chosen = (rows[:, None] - jnp.minimum(first_back, second_back)).astype(jnp.int32)
    half = block_count // 2
    far_block = jnp.where(rows >= half, rows - half, chosen[:, 1]).astype(jnp.int32)
    chosen = chosen.at[:, 1].set(far_block)
    return chosen.at[:, 0].set(rows).astype(jnp.int32)


def shard_levels(stream_key, extent, split, low, high):
    loudness = 1.0
    for axis_at, parts in split:
        heights = jax.random.uniform(jax.random.fold_in(jax.random.fold_in(stream_key, 6), axis_at), (parts,), jnp.float32, low / len(split), high / len(split))
        loudness = loudness * jnp.repeat(jnp.exp(heights), extent[axis_at] // parts).reshape((-1,) + (1,) * (len(extent) - 1 - axis_at))
    return loudness


def length_profile(count, total, reach, skew):
    portions = [(1 << 20) // math.isqrt(grade ** skew) + 1 for grade in range(2, count + 1)]
    surplus, holding = total - reach - (count - 1), [1] * (count - 1)
    while surplus > 0:
        movable = [i for i in range(count - 1) if holding[i] < reach]
        pool, remaining = sum([portions[i] for i in movable]), surplus
        for i in movable:
            extra = min(reach - holding[i], max(1, remaining * portions[i] // pool), surplus)
            holding[i] = holding[i] + extra
            surplus = surplus - extra
    return np.array([reach] + holding)


def uneven_parts(own_key, number_of, total, reach, lean):
    if number_of == 2:
        one = jax.random.randint(own_key, (), max(1, total - reach), min(reach, total - 1) + 1)
        return jnp.stack([one, total - one])
    lengths = jnp.asarray(length_profile(number_of, total, reach, lean), jnp.int32)
    couples = (number_of - 1) // 2
    donor, taker = lengths[1:1 + 2 * couples:2], lengths[2:2 + 2 * couples:2]
    room = jnp.minimum(donor - 1, reach - taker)
    passed = jax.random.randint(jax.random.fold_in(own_key, 1), (couples,), 0, 1 << 20) % (room + 1)
    lengths = lengths.at[1:1 + 2 * couples:2].set(donor - passed).at[2:2 + 2 * couples:2].set(taker + passed)
    return lengths[jax.random.permutation(jax.random.fold_in(own_key, 2), number_of)]


def normal_values(own_key, shape, deviation, reach, cuts=(), kind=jnp.bfloat16):
    array = deviation * jax.random.normal(own_key, shape, jnp.float32)
    if cuts:
        array = array * shard_levels(own_key, shape, cuts, -0.22, 0.18)
    return jnp.clip(array, -reach, reach).astype(kind)


def setup_inputs(seed: int = 0) -> dict:
    splits = jax.random.split(jax.random.key(seed), 11)
    return {
        "t_query": draw_t_query(jax.random.fold_in(splits[10], 71), 0),
        "t_key": draw_t_key(jax.random.fold_in(splits[10], 71), 0),
        "t_value": normal_values(splits[2], (TOKENS, TH * HD), 1.0, 6.0, ((0, 4), (1, 8))),
        "t_out": normal_values(splits[3], (TH * HD, D), (TH * HD) ** -0.5, 0.09375, ((0, 8),)),
        "s_query": draw_s_query(jax.random.fold_in(splits[10], 71), 0),
        "s_key": draw_s_key(jax.random.fold_in(splits[10], 71), 0),
        "s_value": normal_values(splits[6], (TOKENS, SH * HD), 1.0, 6.0, ((0, 4), (1, 8))),
        "s_out": normal_values(splits[7], (SH * HD, D), (SH * HD) ** -0.5, 0.125, ((0, 8),)),
        "segments": jnp.searchsorted(jnp.cumsum(uneven_parts(splits[8], 2, TOKENS, TOKENS - BS, 0)), jnp.arange(TOKENS), side="right").astype(jnp.int32),
        "selection": draw_selection(jax.random.fold_in(splits[10], 71), 0),
    }


masked_score = -1e+30

def teacher_head(queries, key_rows, value_rows, segment_all):
    positions = jnp.arange(queries.shape[0]).astype(jnp.int32)
    scores = jnp.dot(queries, key_rows.T, preferred_element_type=jnp.float32) * HD ** (-0.5)
    allowed = (positions[None, :] <= positions[:, None]) & (segment_all[None, :] == segment_all[:, None])
    scores = jnp.where(allowed, scores, masked_score)
    largest = lax.optimization_barrier(jnp.max(scores, axis=1, keepdims=True))
    weights = jnp.where(allowed, jnp.exp(scores - largest), 0.0)
    running = lax.optimization_barrier(jnp.sum(weights, axis=1, keepdims=True))
    blended = jnp.dot(weights.astype(jnp.bfloat16), value_rows, preferred_element_type=jnp.float32)
    return (blended / running).astype(jnp.bfloat16)

def student_attn(queries, key_all, value_all, segment_all, selection, first_row):
    row_count = queries.shape[0]
    head_count = queries.shape[1] // HD
    blocks = row_count // BS
    query_blocks = queries.reshape(blocks, BS, head_count, HD)
    key_blocks = key_all.reshape(-1, BS, head_count, HD)[selection].reshape(blocks, NSEL * BS, head_count, HD)
    value_blocks = value_all.reshape(-1, BS, head_count, HD)[selection].reshape(blocks, NSEL * BS, head_count, HD)
    key_pos = (selection[:, :, None] * BS + jnp.arange(BS).astype(jnp.int32)[None, None, :]).astype(jnp.int32).reshape(blocks, NSEL * BS)
    query_pos = (first_row + jnp.arange(row_count).astype(jnp.int32)).astype(jnp.int32).reshape(blocks, BS)
    key_seg = segment_all[key_pos]
    query_seg = segment_all[query_pos]
    scores = jnp.einsum('bqhd,bkhd->bhqk', query_blocks, key_blocks, precision=lax.Precision.HIGHEST) * HD ** (-0.5)
    allowed = ((key_pos[:, None, :] <= query_pos[:, :, None]) & (key_seg[:, None, :] == query_seg[:, :, None]))[:, None]
    scores = jnp.where(allowed, scores, masked_score)
    largest = lax.stop_gradient(lax.optimization_barrier(jnp.max(scores, axis=3, keepdims=True)))
    weights = jnp.where(allowed, jnp.exp(scores - largest), 0.0)
    weights = weights / lax.optimization_barrier(jnp.sum(weights, axis=3, keepdims=True))
    blended = jnp.einsum('bhqk,bkhd->bqhd', weights, value_blocks, precision=lax.Precision.HIGHEST)
    return blended.reshape(row_count, head_count * HD)

def reference(t_query, t_key, t_value, t_out, s_query, s_key, s_value, s_out, segments, selection):
    tokens = t_query.shape[0]

    def heads_first(matrix):
        return matrix.reshape(tokens, -1, HD).transpose(1, 0, 2)

    def heads_last(matrix):
        return matrix.transpose(1, 0, 2).reshape(tokens, -1)
    teacher = lax.map(lambda triple: teacher_head(triple[0], triple[1], triple[2], segments), (heads_first(t_query), heads_first(t_key), heads_first(t_value)))
    t_attn = heads_last(teacher)
    student_inputs = (heads_first(s_query.astype(jnp.float32)), heads_first(s_key.astype(jnp.float32)), heads_first(s_value.astype(jnp.float32)))

    def student_forward(triple):
        return student_attn(triple[0], triple[1], triple[2], segments, selection, 0)
    s_attn = heads_last(lax.map(student_forward, student_inputs)).astype(jnp.bfloat16)
    groups = N_HEAD * N_GRP
    teacher_cols = TH * HD // groups
    student_cols = SH * HD // groups
    mismatch = jnp.zeros((tokens, D), jnp.float32)
    for group_index in range(groups):
        student_part = jnp.dot(s_attn[:, group_index * student_cols:(group_index + 1) * student_cols], s_out[group_index * student_cols:(group_index + 1) * student_cols], preferred_element_type=jnp.float32)
        teacher_part = jnp.dot(t_attn[:, group_index * teacher_cols:(group_index + 1) * teacher_cols], t_out[group_index * teacher_cols:(group_index + 1) * teacher_cols], preferred_element_type=jnp.float32)
        rounded = lax.optimization_barrier((student_part - teacher_part).astype(jnp.bfloat16))
        mismatch = mismatch + rounded.astype(jnp.float32)
    grad_out = jnp.dot(mismatch.astype(jnp.bfloat16), s_out.T, preferred_element_type=jnp.float32)

    def student_backward(quadruple):

        def local_attn(first, second, third):
            return student_attn(first, second, third, segments, selection, 0)
        _, pullback = jax.vjp(local_attn, quadruple[0], quadruple[1], quadruple[2])
        return pullback(quadruple[3])
    grad_query, grad_keys, grad_values = lax.map(student_backward, student_inputs + (heads_first(grad_out),))
    return (mismatch, heads_last(grad_query), heads_last(grad_keys), heads_last(grad_values))
```

```python
import functools

import jax
import jax.numpy as jnp
from jax import lax
from jax.experimental import pallas as pl
from jax.experimental.pallas import tpu as pltpu
from jax.sharding import PartitionSpec as P

HD = 128
BS = 64
SCALE = HD ** (-0.5)
LOG2E = 1.4426950408889634
MASKED = -1e30
VMEM_LIMIT = 56 * 1024 * 1024

NT = (((1,), (1,)), ((), ()))
TN = (((0,), (0,)), ((), ()))


def dot(a, b, dims=(((1,), (0,)), ((), ()))):
    return lax.dot_general(a, b, dims, preferred_element_type=jnp.float32)


def visible(key_pos, query_pos, first_count):
    low = jnp.where(query_pos < first_count, 0, first_count)
    return (key_pos <= query_pos) & (key_pos >= low)


def teacher_kernel(tile, info_ref, q_ref, k_ref, v_ref, o_ref):
    offset, first_count = info_ref[0], info_ref[1]
    q_tile = q_ref.shape[0]
    q_start = offset + pl.program_id(1) * q_tile
    q_end = q_start + q_tile
    queries = q_ref[...]

    def step(index, carried, masked):
        largest, total, acc = carried
        rows = pl.ds(pl.multiple_of(index * tile, tile), tile)
        scores = dot(k_ref[rows, :], queries, NT)
        if masked:
            key_pos = index * tile + lax.broadcasted_iota(jnp.int32, scores.shape, 0)
            query_pos = q_start + lax.broadcasted_iota(jnp.int32, (1, q_tile), 1)
            scores = jnp.where(visible(key_pos, query_pos, first_count), scores, MASKED)
        new = jnp.maximum(largest, jnp.max(scores, axis=0, keepdims=True))
        weights = jnp.exp2((scores - new) * (SCALE * LOG2E))
        if masked:
            weights = jnp.where(scores > 0.5 * MASKED, weights, 0.0)
        factor = jnp.exp2((largest - new) * (SCALE * LOG2E))
        total = total * factor + jnp.sum(weights, axis=0, keepdims=True)
        acc = acc * factor + dot(v_ref[rows, :], weights.astype(jnp.bfloat16), TN)
        return new, total, acc

    first = jnp.where(q_start >= first_count, first_count // tile, 0)
    last = (q_end + tile - 1) // tile
    straddles = first_count < q_end

    def general(index, carried):
        low, high = index * tile, (index + 1) * tile
        need = (high > q_start) | ((low < first_count) & straddles)
        return lax.cond(
            need,
            lambda c: step(index, c, True),
            lambda c: step(index, c, False),
            carried,
        )

    carried = (
        jnp.full((1, q_tile), MASKED, jnp.float32),
        jnp.zeros((1, q_tile), jnp.float32),
        jnp.zeros((HD, q_tile), jnp.float32),
    )
    _, total, acc = lax.fori_loop(first, last, general, carried)
    o_ref[...] = (acc / total).T.astype(jnp.bfloat16)


def teacher(queries, keys, values, offset, first_count):
    rows, width = queries.shape
    tokens = keys.shape[0]
    heads = width // HD
    tile = 512
    info = jnp.stack([offset, first_count]).astype(jnp.int32)
    return pl.pallas_call(
        functools.partial(teacher_kernel, tile),
        grid_spec=pltpu.PrefetchScalarGridSpec(
            num_scalar_prefetch=1,
            grid=(heads, rows // tile),
            in_specs=[
                pl.BlockSpec((tile, HD), lambda h, i, s: (i, h)),
                pl.BlockSpec((tokens, HD), lambda h, i, s: (0, h)),
                pl.BlockSpec((tokens, HD), lambda h, i, s: (0, h)),
            ],
            out_specs=pl.BlockSpec((tile, HD), lambda h, i, s: (i, h)),
        ),
        out_shape=jax.ShapeDtypeStruct((rows, width), jnp.bfloat16),
        compiler_params=pltpu.CompilerParams(vmem_limit_bytes=VMEM_LIMIT),
        cost_estimate=pl.CostEstimate(
            flops=2 * rows * tokens * width, bytes_accessed=8 * tokens * width, transcendentals=0
        ),
    )(info, queries, keys, values)


def spread(ref, scratch, heads):
    for h in range(heads):
        cols = slice(h * HD, (h + 1) * HD)
        scratch[h * BS : (h + 1) * BS, cols] = ref[:, cols].astype(scratch.dtype)


def student_weights(sel_ref, info_ref, q_wide, k_all, v_all, k_sel, v_sel, pos, heads):
    block = pl.program_id(0)
    count = sel_ref.shape[1]
    offset, first_count = info_ref[0], info_ref[1]
    within = lax.broadcasted_iota(jnp.int32, (BS, 1), 0)
    for e in range(count):
        chosen = sel_ref[block, e]
        source = pl.ds(pl.multiple_of(chosen * BS, BS), BS)
        k_sel[e * BS : (e + 1) * BS, :] = k_all[source, :]
        v_sel[e * BS : (e + 1) * BS, :] = v_all[source, :]
        pos[e * BS : (e + 1) * BS, :] = jnp.broadcast_to(chosen * BS + within, (BS, heads * BS))
    lane = lax.broadcasted_iota(jnp.int32, (1, heads * BS), 1)
    query_pos = offset + block * BS + lax.rem(lane, BS)
    scores = dot(k_sel[...], q_wide[...], NT)
    allowed = visible(pos[...], query_pos, first_count)
    scores = jnp.where(allowed, scores, MASKED)
    largest = jnp.max(scores, axis=0, keepdims=True)
    weights = jnp.exp2((scores - largest) * (SCALE * LOG2E))
    weights = jnp.where(allowed, weights, 0.0)
    return weights, jnp.sum(weights, axis=0, keepdims=True)


def forward_kernel(heads, sel_ref, info_ref, q_ref, k_all, v_all, o_ref, q_wide, k_sel, v_sel, pos):
    @pl.when(pl.program_id(0) == 0)
    def _():
        q_wide[...] = jnp.zeros_like(q_wide)

    spread(q_ref, q_wide, heads)
    weights, total = student_weights(
        sel_ref, info_ref, q_wide, k_all, v_all, k_sel, v_sel, pos, heads
    )
    weights = (weights / total).astype(jnp.bfloat16)
    blended = dot(weights, v_sel[...], TN)
    for h in range(heads):
        cols = slice(h * HD, (h + 1) * HD)
        o_ref[:, cols] = blended[h * BS : (h + 1) * BS, cols].astype(jnp.bfloat16)


def backward_kernel(
    heads, sel_ref, info_ref, q_ref, g_ref, k_all, v_all, dq_ref, dk_ref, dv_ref,
    q_wide, g_wide, k_sel, v_sel, pos,
):
    @pl.when(pl.program_id(0) == 0)
    def _():
        q_wide[...] = jnp.zeros_like(q_wide)
        g_wide[...] = jnp.zeros_like(g_wide)
        dk_ref[...] = jnp.zeros_like(dk_ref)
        dv_ref[...] = jnp.zeros_like(dv_ref)

    spread(q_ref, q_wide, heads)
    spread(g_ref, g_wide, heads)
    weights, total = student_weights(
        sel_ref, info_ref, q_wide, k_all, v_all, k_sel, v_sel, pos, heads
    )
    weights = weights / total
    weight_grad = dot(v_sel[...], g_wide[...], NT)
    row_dots = jnp.sum(weights * weight_grad, axis=0, keepdims=True)
    score_grad = (weights * (weight_grad - row_dots) * SCALE).astype(jnp.bfloat16)
    query_grad = dot(score_grad, k_sel[...], TN)
    for h in range(heads):
        cols = slice(h * HD, (h + 1) * HD)
        dq_ref[:, cols] = query_grad[h * BS : (h + 1) * BS, cols]
    key_grad = dot(score_grad, q_wide[...])
    value_grad = dot(weights.astype(jnp.bfloat16), g_wide[...])
    block = pl.program_id(0)
    for e in range(sel_ref.shape[1]):
        target = pl.ds(pl.multiple_of(sel_ref[block, e] * BS, BS), BS)
        dk_ref[target, :] += key_grad[e * BS : (e + 1) * BS, :]
        dv_ref[target, :] += value_grad[e * BS : (e + 1) * BS, :]


def student_scratch(heads, keys, wides):
    width = heads * HD
    return [pltpu.VMEM((heads * BS, width), jnp.bfloat16)] * wides + [
        pltpu.VMEM((keys, width), jnp.bfloat16),
        pltpu.VMEM((keys, width), jnp.bfloat16),
        pltpu.VMEM((keys, heads * BS), jnp.int32),
    ]


def student_forward(selection, info, queries, keys, values):
    rows, width = queries.shape
    tokens = keys.shape[0]
    heads = width // HD
    row_block = pl.BlockSpec((BS, width), lambda b, *_: (b, 0))
    whole = pl.BlockSpec((tokens, width), lambda b, *_: (0, 0))
    return pl.pallas_call(
        functools.partial(forward_kernel, heads),
        grid_spec=pltpu.PrefetchScalarGridSpec(
            num_scalar_prefetch=2,
            grid=(rows // BS,),
            in_specs=[row_block, whole, whole],
            out_specs=row_block,
            scratch_shapes=student_scratch(heads, selection.shape[1] * BS, 1),
        ),
        out_shape=jax.ShapeDtypeStruct((rows, width), jnp.bfloat16),
        compiler_params=pltpu.CompilerParams(vmem_limit_bytes=VMEM_LIMIT),
        cost_estimate=pl.CostEstimate(
            flops=16 * rows * tokens * width, bytes_accessed=4 * tokens * width, transcendentals=0
        ),
    )(selection, info, queries, keys, values)


def student_backward(selection, info, queries, grads, keys, values):
    rows, width = queries.shape
    tokens = keys.shape[0]
    heads = width // HD
    row_block = pl.BlockSpec((BS, width), lambda b, *_: (b, 0))
    whole = pl.BlockSpec((tokens, width), lambda b, *_: (0, 0))
    return pl.pallas_call(
        functools.partial(backward_kernel, heads),
        grid_spec=pltpu.PrefetchScalarGridSpec(
            num_scalar_prefetch=2,
            grid=(rows // BS,),
            in_specs=[row_block, row_block, whole, whole],
            out_specs=[row_block, whole, whole],
            scratch_shapes=student_scratch(heads, selection.shape[1] * BS, 2),
        ),
        out_shape=[
            jax.ShapeDtypeStruct((rows, width), jnp.float32),
            jax.ShapeDtypeStruct((tokens, width), jnp.float32),
            jax.ShapeDtypeStruct((tokens, width), jnp.float32),
        ],
        compiler_params=pltpu.CompilerParams(vmem_limit_bytes=VMEM_LIMIT),
    )(selection, info, queries, grads, keys, values)


def project_kernel(s_attn, t_attn, s_out, t_out, o_ref):
    o_ref[0] = (dot(s_attn[...], s_out[...]) - dot(t_attn[...], t_out[...])).astype(jnp.bfloat16)


def project(s_attn, t_attn, s_out, t_out, groups):
    rows = s_attn.shape[0]
    model = s_out.shape[1]
    tile = model // groups
    return pl.pallas_call(
        project_kernel,
        grid=(groups,),
        in_specs=[
            pl.BlockSpec(s_attn.shape, lambda j: (0, 0)),
            pl.BlockSpec(t_attn.shape, lambda j: (0, 0)),
            pl.BlockSpec((s_out.shape[0], tile), lambda j: (0, j)),
            pl.BlockSpec((t_out.shape[0], tile), lambda j: (0, j)),
        ],
        out_specs=pl.BlockSpec((1, rows, tile), lambda j: (j, 0, 0)),
        out_shape=jax.ShapeDtypeStruct((groups, rows, tile), jnp.bfloat16),
        compiler_params=pltpu.CompilerParams(vmem_limit_bytes=VMEM_LIMIT),
    )(s_attn, t_attn, s_out, t_out)


def gradient_kernel(m_ref, w_ref, o_ref):
    part = dot(m_ref[0], w_ref[...], NT)

    @pl.when(pl.program_id(0) == 0)
    def _():
        o_ref[...] = part

    @pl.when(pl.program_id(0) > 0)
    def _():
        o_ref[...] += part


def gradient(mismatch, s_out):
    groups, rows, tile = mismatch.shape
    width = s_out.shape[0]
    return pl.pallas_call(
        gradient_kernel,
        grid=(groups,),
        in_specs=[
            pl.BlockSpec((1, rows, tile), lambda j: (j, 0, 0)),
            pl.BlockSpec((width, tile), lambda j: (0, j)),
        ],
        out_specs=pl.BlockSpec((rows, width), lambda j: (0, 0)),
        out_shape=jax.ShapeDtypeStruct((rows, width), jnp.float32),
        compiler_params=pltpu.CompilerParams(vmem_limit_bytes=VMEM_LIMIT),
    )(mismatch, s_out)


def on_device(t_query, t_key, t_value, t_out, s_query, s_key, s_value, s_out, segments, selection):
    row_count = t_query.shape[0]
    heads = t_query.shape[1] // HD
    cycle = lax.axis_size("blk")
    groups = lax.axis_size("head") * lax.axis_size("grp")
    my_index = lax.axis_index("blk")
    first_row = my_index * row_count

    first_count = lax.psum(jnp.sum((segments == 0).astype(jnp.int32)), "blk")
    info = jnp.stack([first_row, first_count]).astype(jnp.int32)

    if heads % cycle == 0:
        def by_head(rows):
            return lax.all_to_all(rows, "blk", split_axis=1, concat_axis=0, tiled=True)

        whole_heads = teacher(
            by_head(t_query), by_head(t_key), by_head(t_value), jnp.int32(0), first_count
        )
        t_attn = lax.all_to_all(whole_heads, "blk", split_axis=0, concat_axis=1, tiled=True)
    else:
        t_attn = teacher(
            t_query,
            lax.all_gather(t_key, "blk", axis=0, tiled=True),
            lax.all_gather(t_value, "blk", axis=0, tiled=True),
            first_row,
            first_count,
        )

    key_full = lax.all_gather(s_key, "blk", axis=0, tiled=True)
    value_full = lax.all_gather(s_value, "blk", axis=0, tiled=True)
    s_attn = student_forward(selection, info, s_query, key_full, value_full)

    terms = project(s_attn, t_attn, s_out, t_out, groups)
    mismatch = lax.psum_scatter(terms, ("head", "grp"), scatter_dimension=0, tiled=False)
    grad_attn = gradient(lax.all_gather(mismatch, ("head", "grp"), axis=0, tiled=False), s_out)
    grad_query, grad_keys, grad_values = student_backward(
        selection, info, s_query, grad_attn, key_full, value_full
    )

    def own(full, index):
        return lax.dynamic_slice_in_dim(full, index * row_count, row_count, 0)

    key_grads, value_grads = own(grad_keys, my_index), own(grad_values, my_index)
    for distance in range(1, cycle):
        owner = jnp.maximum(my_index - distance, 0)
        route = [(i, i - distance) for i in range(distance, cycle)]
        for_keys = lax.ppermute(own(grad_keys, owner).astype(jnp.bfloat16), "blk", route)
        for_values = lax.ppermute(own(grad_values, owner).astype(jnp.bfloat16), "blk", route)
        key_grads = key_grads + for_keys.astype(jnp.float32)
        value_grads = value_grads + for_values.astype(jnp.float32)
    return (mismatch.astype(jnp.float32), grad_query, key_grads, value_grads)


def solution(mesh):
    split = ("head", "grp")
    tokens, weights = P("blk", split), P(split, None)
    return jax.shard_map(
        on_device,
        mesh=mesh,
        in_specs=(
            tokens, tokens, tokens, weights, tokens, tokens, tokens, weights, P("blk"),
            P("blk", None),
        ),
        out_specs=(tokens,) * 4,
        check_vma=False,
    )
```

```python
import functools

import jax
import jax.numpy as jnp
from jax import lax
from jax.experimental import pallas as pl
from jax.experimental.pallas import tpu as pltpu
from jax.sharding import PartitionSpec as P

HD = 128
BS = 64
SCALE = HD ** (-0.5)
LOG2E = 1.4426950408889634
MASKED = -1e30
VMEM_LIMIT = 56 * 1024 * 1024

NT = (((1,), (1,)), ((), ()))
TN = (((0,), (0,)), ((), ()))


def dot(a, b, dims=(((1,), (0,)), ((), ()))):
    return lax.dot_general(a, b, dims, preferred_element_type=jnp.float32)


def visible(key_pos, query_pos, first_count):
    low = jnp.where(query_pos < first_count, 0, first_count)
    return (key_pos <= query_pos) & (key_pos >= low)


def teacher_kernel(tile, info_ref, q_ref, k_ref, v_ref, o_ref):
    offset, first_count = info_ref[0], info_ref[1]
    q_tile = q_ref.shape[0]
    q_start = offset + pl.program_id(1) * q_tile
    q_end = q_start + q_tile
    queries = q_ref[...]

    def step(index, carried, masked):
        largest, total, acc = carried
        rows = pl.ds(pl.multiple_of(index * tile, tile), tile)
        scores = dot(k_ref[rows, :], queries, NT)
        if masked:
            key_pos = index * tile + lax.broadcasted_iota(jnp.int32, scores.shape, 0)
            query_pos = q_start + lax.broadcasted_iota(jnp.int32, (1, q_tile), 1)
            scores = jnp.where(visible(key_pos, query_pos, first_count), scores, MASKED)
        new = jnp.maximum(largest, jnp.max(scores, axis=0, keepdims=True))
        weights = jnp.exp2((scores - new) * (SCALE * LOG2E))
        if masked:
            weights = jnp.where(scores > 0.5 * MASKED, weights, 0.0)
        factor = jnp.exp2((largest - new) * (SCALE * LOG2E))
        total = total * factor + jnp.sum(weights, axis=0, keepdims=True)
        acc = acc * factor + dot(v_ref[rows, :], weights.astype(jnp.bfloat16), TN)
        return new, total, acc

    first = jnp.where(q_start >= first_count, first_count // tile, 0)
    last = (q_end + tile - 1) // tile
    straddles = first_count < q_end

    def general(index, carried):
        low, high = index * tile, (index + 1) * tile
        need = (high > q_start) | ((low < first_count) & straddles)
        return lax.cond(
            need,
            lambda c: step(index, c, True),
            lambda c: step(index, c, False),
            carried,
        )

    carried = (
        jnp.full((1, q_tile), MASKED, jnp.float32),
        jnp.zeros((1, q_tile), jnp.float32),
        jnp.zeros((HD, q_tile), jnp.float32),
    )
    _, total, acc = lax.fori_loop(first, last, general, carried)
    o_ref[...] = (acc / total).T.astype(jnp.bfloat16)


def teacher(queries, keys, values, offset, first_count):
    rows, width = queries.shape
    tokens = keys.shape[0]
    heads = width // HD
    tile = 512
    info = jnp.stack([offset, first_count]).astype(jnp.int32)
    return pl.pallas_call(
        functools.partial(teacher_kernel, tile),
        grid_spec=pltpu.PrefetchScalarGridSpec(
            num_scalar_prefetch=1,
            grid=(heads, rows // tile),
            in_specs=[
                pl.BlockSpec((tile, HD), lambda h, i, s: (i, h)),
                pl.BlockSpec((tokens, HD), lambda h, i, s: (0, h)),
                pl.BlockSpec((tokens, HD), lambda h, i, s: (0, h)),
            ],
            out_specs=pl.BlockSpec((tile, HD), lambda h, i, s: (i, h)),
        ),
        out_shape=jax.ShapeDtypeStruct((rows, width), jnp.bfloat16),
        compiler_params=pltpu.CompilerParams(vmem_limit_bytes=VMEM_LIMIT),
        cost_estimate=pl.CostEstimate(
            flops=2 * rows * tokens * width, bytes_accessed=8 * tokens * width, transcendentals=0
        ),
    )(info, queries, keys, values)


def spread(ref, scratch, heads):
    for h in range(heads):
        cols = slice(h * HD, (h + 1) * HD)
        scratch[h * BS : (h + 1) * BS, cols] = ref[:, cols].astype(scratch.dtype)


def student_weights(sel_ref, place_ref, info_ref, q_wide, k_all, v_all, k_sel, v_sel, pos, heads):
    block = pl.program_id(0)
    count = sel_ref.shape[1]
    offset, first_count = info_ref[0], info_ref[1]
    within = lax.broadcasted_iota(jnp.int32, (BS, 1), 0)
    for e in range(count):
        chosen = sel_ref[block, e]
        source = pl.ds(pl.multiple_of(place_ref[block, e] * BS, BS), BS)
        k_sel[e * BS : (e + 1) * BS, :] = k_all[source, :]
        v_sel[e * BS : (e + 1) * BS, :] = v_all[source, :]
        pos[e * BS : (e + 1) * BS, :] = jnp.broadcast_to(chosen * BS + within, (BS, heads * BS))
    lane = lax.broadcasted_iota(jnp.int32, (1, heads * BS), 1)
    query_pos = offset + block * BS + lax.rem(lane, BS)
    scores = dot(k_sel[...], q_wide[...], NT)
    allowed = visible(pos[...], query_pos, first_count)
    scores = jnp.where(allowed, scores, MASKED)
    largest = jnp.max(scores, axis=0, keepdims=True)
    weights = jnp.exp2((scores - largest) * (SCALE * LOG2E))
    weights = jnp.where(allowed, weights, 0.0)
    return weights, jnp.sum(weights, axis=0, keepdims=True)


def forward_kernel(heads, sel_ref, place_ref, info_ref, q_ref, k_all, v_all, o_ref, q_wide, k_sel, v_sel, pos):
    @pl.when(pl.program_id(0) == 0)
    def _():
        q_wide[...] = jnp.zeros_like(q_wide)

    spread(q_ref, q_wide, heads)
    weights, total = student_weights(
        sel_ref, place_ref, info_ref, q_wide, k_all, v_all, k_sel, v_sel, pos, heads
    )
    weights = (weights / total).astype(jnp.bfloat16)
    blended = dot(weights, v_sel[...], TN)
    for h in range(heads):
        cols = slice(h * HD, (h + 1) * HD)
        o_ref[:, cols] = blended[h * BS : (h + 1) * BS, cols].astype(jnp.bfloat16)


def backward_kernel(
    heads, cycle, sel_ref, place_ref, info_ref, q_ref, g_ref, k_all, v_all, dq_ref, *rest
):
    own_ref, far_refs = rest[0], rest[1:cycle]
    dk_sum, dv_sum, q_wide, g_wide, k_sel, v_sel, pos = rest[cycle:]
    block = pl.program_id(0)

    @pl.when(block == 0)
    def _():
        q_wide[...] = jnp.zeros_like(q_wide)
        g_wide[...] = jnp.zeros_like(g_wide)
        dk_sum[...] = jnp.zeros_like(dk_sum)
        dv_sum[...] = jnp.zeros_like(dv_sum)

    spread(q_ref, q_wide, heads)
    spread(g_ref, g_wide, heads)
    weights, total = student_weights(
        sel_ref, place_ref, info_ref, q_wide, k_all, v_all, k_sel, v_sel, pos, heads
    )
    weights = weights / total
    weight_grad = dot(v_sel[...], g_wide[...], NT)
    row_dots = jnp.sum(weights * weight_grad, axis=0, keepdims=True)
    score_grad = (weights * (weight_grad - row_dots) * SCALE).astype(jnp.bfloat16)
    query_grad = dot(score_grad, k_sel[...], TN)
    for h in range(heads):
        cols = slice(h * HD, (h + 1) * HD)
        dq_ref[:, cols] = query_grad[h * BS : (h + 1) * BS, cols]
    key_grad = dot(score_grad, q_wide[...])
    value_grad = dot(weights.astype(jnp.bfloat16), g_wide[...])
    for e in range(sel_ref.shape[1]):
        target = pl.ds(pl.multiple_of(place_ref[block, e] * BS, BS), BS)
        dk_sum[target, :] += key_grad[e * BS : (e + 1) * BS, :]
        dv_sum[target, :] += value_grad[e * BS : (e + 1) * BS, :]

    @pl.when(block == pl.num_programs(0) - 1)
    def _():
        rows = own_ref.shape[1]
        own_ref[0] = dk_sum[:rows, :]
        own_ref[1] = dv_sum[:rows, :]
        for d in range(1, cycle):
            far_refs[d - 1][0] = dk_sum[d * rows : (d + 1) * rows, :].astype(jnp.bfloat16)
            far_refs[d - 1][1] = dv_sum[d * rows : (d + 1) * rows, :].astype(jnp.bfloat16)


def student_scratch(heads, keys, wides):
    width = heads * HD
    return [pltpu.VMEM((heads * BS, width), jnp.bfloat16)] * wides + [
        pltpu.VMEM((keys, width), jnp.bfloat16),
        pltpu.VMEM((keys, width), jnp.bfloat16),
        pltpu.VMEM((keys, heads * BS), jnp.int32),
    ]


def student_forward(tables, queries, keys, values):
    rows, width = queries.shape
    tokens = keys.shape[0]
    heads = width // HD
    row_block = pl.BlockSpec((BS, width), lambda b, *_: (b, 0))
    whole = pl.BlockSpec((tokens, width), lambda b, *_: (0, 0))
    return pl.pallas_call(
        functools.partial(forward_kernel, heads),
        grid_spec=pltpu.PrefetchScalarGridSpec(
            num_scalar_prefetch=3,
            grid=(rows // BS,),
            in_specs=[row_block, whole, whole],
            out_specs=row_block,
            scratch_shapes=student_scratch(heads, tables[0].shape[1] * BS, 1),
        ),
        out_shape=jax.ShapeDtypeStruct((rows, width), jnp.bfloat16),
        compiler_params=pltpu.CompilerParams(vmem_limit_bytes=VMEM_LIMIT),
        cost_estimate=pl.CostEstimate(
            flops=16 * rows * tokens * width, bytes_accessed=4 * tokens * width, transcendentals=0
        ),
    )(*tables, queries, keys, values)


def student_backward(tables, queries, grads, keys, values):
    rows, width = queries.shape
    tokens = keys.shape[0]
    cycle = tokens // rows
    heads = width // HD
    row_block = pl.BlockSpec((BS, width), lambda b, *_: (b, 0))
    whole = pl.BlockSpec((tokens, width), lambda b, *_: (0, 0))
    pair = pl.BlockSpec((2, rows, width), lambda b, *_: (0, 0, 0))
    return pl.pallas_call(
        functools.partial(backward_kernel, heads, cycle),
        grid_spec=pltpu.PrefetchScalarGridSpec(
            num_scalar_prefetch=3,
            grid=(rows // BS,),
            in_specs=[row_block, row_block, whole, whole],
            out_specs=[row_block] + [pair] * cycle,
            scratch_shapes=[pltpu.VMEM((tokens, width), jnp.float32)] * 2
            + student_scratch(heads, tables[0].shape[1] * BS, 2),
        ),
        out_shape=[
            jax.ShapeDtypeStruct((rows, width), jnp.float32),
            jax.ShapeDtypeStruct((2, rows, width), jnp.float32),
        ]
        + [jax.ShapeDtypeStruct((2, rows, width), jnp.bfloat16)] * (cycle - 1),
        compiler_params=pltpu.CompilerParams(vmem_limit_bytes=VMEM_LIMIT),
        cost_estimate=pl.CostEstimate(
            flops=32 * rows * tokens * width, bytes_accessed=8 * tokens * width, transcendentals=0
        ),
    )(*tables, queries, grads, keys, values)


def project_kernel(s_attn, t_attn, s_out, t_out, o_ref):
    o_ref[0] = (dot(s_attn[...], s_out[...]) - dot(t_attn[...], t_out[...])).astype(jnp.bfloat16)


def project(s_attn, t_attn, s_out, t_out, groups):
    rows = s_attn.shape[0]
    model = s_out.shape[1]
    tile = model // groups
    return pl.pallas_call(
        project_kernel,
        grid=(groups,),
        in_specs=[
            pl.BlockSpec(s_attn.shape, lambda j: (0, 0)),
            pl.BlockSpec(t_attn.shape, lambda j: (0, 0)),
            pl.BlockSpec((s_out.shape[0], tile), lambda j: (0, j)),
            pl.BlockSpec((t_out.shape[0], tile), lambda j: (0, j)),
        ],
        out_specs=pl.BlockSpec((1, rows, tile), lambda j: (j, 0, 0)),
        out_shape=jax.ShapeDtypeStruct((groups, rows, tile), jnp.bfloat16),
        compiler_params=pltpu.CompilerParams(vmem_limit_bytes=VMEM_LIMIT),
    )(s_attn, t_attn, s_out, t_out)


def from_earlier(rows, distance):
    route = [(i - distance, i) for i in range(distance, lax.axis_size("blk"))]
    return lax.ppermute(rows, "blk", route)


def on_device(t_query, t_key, t_value, t_out, s_query, s_key, s_value, s_out, segments, selection):
    row_count = t_query.shape[0]
    heads = t_query.shape[1] // HD
    cycle = lax.axis_size("blk")
    split = ("head", "grp")
    groups = lax.axis_size("head") * lax.axis_size("grp")
    my_index = lax.axis_index("blk")
    first_row = my_index * row_count
    shard_blocks = row_count // BS

    count = jnp.sum((segments == 0).astype(jnp.int32)).reshape(1)
    first_count = count
    for distance in range(1, cycle):
        route = [(i, (i + distance) % cycle) for i in range(cycle)]
        first_count = first_count + lax.ppermute(count, "blk", route)
    first_count = first_count[0]
    info = jnp.stack([first_row, first_count]).astype(jnp.int32)

    mixed = []
    for h in range(s_out.shape[0] // HD):
        part = lax.all_gather(s_out[h * HD : (h + 1) * HD, :], split, axis=0, tiled=True)
        mixed.append(
            (dot(s_out, part, NT).astype(jnp.bfloat16), dot(t_out, part, NT).astype(jnp.bfloat16))
        )

    if heads % cycle == 0:
        def by_head(rows):
            return lax.all_to_all(rows, "blk", split_axis=1, concat_axis=0, tiled=True)

        whole_heads = teacher(
            by_head(t_query), by_head(t_key), by_head(t_value), jnp.int32(0), first_count
        )
        t_attn = lax.all_to_all(whole_heads, "blk", split_axis=0, concat_axis=1, tiled=True)
    else:
        t_attn = teacher(
            t_query,
            lax.all_gather(t_key, "blk", axis=0, tiled=True),
            lax.all_gather(t_value, "blk", axis=0, tiled=True),
            first_row,
            first_count,
        )

    key_stack = jnp.concatenate([s_key] + [from_earlier(s_key, d) for d in range(1, cycle)])
    value_stack = jnp.concatenate([s_value] + [from_earlier(s_value, d) for d in range(1, cycle)])
    place = (my_index - selection // shard_blocks) * shard_blocks + selection % shard_blocks
    tables = (selection, place, info)
    s_attn = student_forward(tables, s_query, key_stack, value_stack)

    grads = []
    for s_mix, t_mix in mixed:
        terms = project(s_attn, t_attn, s_mix, t_mix, groups)
        grads.append(lax.psum_scatter(terms, split, scatter_dimension=0, tiled=False))
    terms = project(s_attn, t_attn, s_out, t_out, groups)
    terms, grads = lax.optimization_barrier((terms, grads))
    mismatch = lax.psum_scatter(terms, split, scatter_dimension=0, tiled=False)

    grad_query, own, *far = student_backward(
        tables, s_query, jnp.concatenate(grads, axis=1), key_stack, value_stack
    )
    for distance in range(1, cycle):
        route = [(i, i - distance) for i in range(distance, cycle)]
        own = own + lax.ppermute(far[distance - 1], "blk", route).astype(jnp.float32)
    return (mismatch.astype(jnp.float32), grad_query, own[0], own[1])


def solution(mesh):
    split = ("head", "grp")
    tokens, weights = P("blk", split), P(split, None)
    return jax.shard_map(
        on_device,
        mesh=mesh,
        in_specs=(
            tokens, tokens, tokens, weights, tokens, tokens, tokens, weights, P("blk"),
            P("blk", None),
        ),
        out_specs=(tokens,) * 4,
        check_vma=False,
    )
```

```python
import functools

import jax
import jax.numpy as jnp
from jax import lax
from jax.experimental import pallas as pl
from jax.experimental.pallas import tpu as pltpu
from jax.sharding import PartitionSpec as P

HD = 128
BS = 64
SCALE = HD ** (-0.5)
LOG2E = 1.4426950408889634
MASKED = -1e30
VMEM_LIMIT = 56 * 1024 * 1024

NT = (((1,), (1,)), ((), ()))
TN = (((0,), (0,)), ((), ()))


def dot(a, b, dims=(((1,), (0,)), ((), ()))):
    return lax.dot_general(a, b, dims, preferred_element_type=jnp.float32)


def visible(key_pos, query_pos, first_count):
    low = jnp.where(query_pos < first_count, 0, first_count)
    return (key_pos <= query_pos) & (key_pos >= low)


def teacher_kernel(tile, info_ref, q_ref, k_ref, v_ref, o_ref):
    offset, first_count = info_ref[0], info_ref[1]
    q_tile = q_ref.shape[0]
    q_start = offset + pl.program_id(1) * q_tile
    q_end = q_start + q_tile
    queries = q_ref[...]

    def step(index, carried, masked):
        largest, total, acc = carried
        rows = pl.ds(pl.multiple_of(index * tile, tile), tile)
        scores = dot(k_ref[rows, :], queries, NT)
        if masked:
            key_pos = index * tile + lax.broadcasted_iota(jnp.int32, scores.shape, 0)
            query_pos = q_start + lax.broadcasted_iota(jnp.int32, (1, q_tile), 1)
            scores = jnp.where(visible(key_pos, query_pos, first_count), scores, MASKED)
        new = jnp.maximum(largest, jnp.max(scores, axis=0, keepdims=True))
        weights = jnp.exp2((scores - new) * (SCALE * LOG2E))
        if masked:
            weights = jnp.where(scores > 0.5 * MASKED, weights, 0.0)
        factor = jnp.exp2((largest - new) * (SCALE * LOG2E))
        total = total * factor + jnp.sum(weights, axis=0, keepdims=True)
        acc = acc * factor + dot(v_ref[rows, :], weights.astype(jnp.bfloat16), TN)
        return new, total, acc

    first = jnp.where(q_start >= first_count, first_count // tile, 0)
    last = (q_end + tile - 1) // tile
    straddles = first_count < q_end

    def general(index, carried):
        low, high = index * tile, (index + 1) * tile
        need = (high > q_start) | ((low < first_count) & straddles)
        return lax.cond(
            need,
            lambda c: step(index, c, True),
            lambda c: step(index, c, False),
            carried,
        )

    carried = (
        jnp.full((1, q_tile), MASKED, jnp.float32),
        jnp.zeros((1, q_tile), jnp.float32),
        jnp.zeros((HD, q_tile), jnp.float32),
    )
    _, total, acc = lax.fori_loop(first, last, general, carried)
    o_ref[...] = (acc / total).T.astype(jnp.bfloat16)


def teacher(queries, keys, values, heads, columns, offset, first_count):
    rows, tokens = queries.shape[0], keys.shape[0]
    width = heads * HD
    step, (q_at, k_at, v_at) = columns
    tile = 512
    info = jnp.stack([offset, first_count]).astype(jnp.int32)
    return pl.pallas_call(
        functools.partial(teacher_kernel, tile),
        grid_spec=pltpu.PrefetchScalarGridSpec(
            num_scalar_prefetch=1,
            grid=(heads, rows // tile),
            in_specs=[
                pl.BlockSpec((tile, HD), lambda h, i, s: (i, step * h + q_at)),
                pl.BlockSpec((tokens, HD), lambda h, i, s: (0, step * h + k_at)),
                pl.BlockSpec((tokens, HD), lambda h, i, s: (0, step * h + v_at)),
            ],
            out_specs=pl.BlockSpec((tile, HD), lambda h, i, s: (i, h)),
        ),
        out_shape=jax.ShapeDtypeStruct((rows, width), jnp.bfloat16),
        compiler_params=pltpu.CompilerParams(vmem_limit_bytes=VMEM_LIMIT),
        cost_estimate=pl.CostEstimate(
            flops=2 * rows * tokens * width, bytes_accessed=8 * tokens * width, transcendentals=0
        ),
    )(info, queries, keys, values)


def spread(ref, scratch, heads):
    for h in range(heads):
        cols = slice(h * HD, (h + 1) * HD)
        scratch[h * BS : (h + 1) * BS, cols] = ref[:, cols].astype(scratch.dtype)


def student_weights(sel_ref, place_ref, info_ref, q_wide, k_all, v_all, k_sel, v_sel, pos, heads):
    block = pl.program_id(0)
    count = sel_ref.shape[1]
    offset, first_count = info_ref[0], info_ref[1]
    within = lax.broadcasted_iota(jnp.int32, (BS, 1), 0)
    for e in range(count):
        chosen = sel_ref[block, e]
        source = pl.ds(pl.multiple_of(place_ref[block, e] * BS, BS), BS)
        k_sel[e * BS : (e + 1) * BS, :] = k_all[source, :]
        v_sel[e * BS : (e + 1) * BS, :] = v_all[source, :]
        pos[e * BS : (e + 1) * BS, :] = jnp.broadcast_to(chosen * BS + within, (BS, heads * BS))
    lane = lax.broadcasted_iota(jnp.int32, (1, heads * BS), 1)
    query_pos = offset + block * BS + lax.rem(lane, BS)
    scores = dot(k_sel[...], q_wide[...], NT)
    allowed = visible(pos[...], query_pos, first_count)
    scores = jnp.where(allowed, scores, MASKED)
    largest = jnp.max(scores, axis=0, keepdims=True)
    weights = jnp.exp2((scores - largest) * (SCALE * LOG2E))
    weights = jnp.where(allowed, weights, 0.0)
    return weights, jnp.sum(weights, axis=0, keepdims=True)


def forward_kernel(heads, sel_ref, place_ref, info_ref, q_ref, k_all, v_all, o_ref, q_wide, k_sel, v_sel, pos):
    @pl.when(pl.program_id(0) == 0)
    def _():
        q_wide[...] = jnp.zeros_like(q_wide)

    spread(q_ref, q_wide, heads)
    weights, total = student_weights(
        sel_ref, place_ref, info_ref, q_wide, k_all, v_all, k_sel, v_sel, pos, heads
    )
    weights = (weights / total).astype(jnp.bfloat16)
    blended = dot(weights, v_sel[...], TN)
    for h in range(heads):
        cols = slice(h * HD, (h + 1) * HD)
        o_ref[:, cols] = blended[h * BS : (h + 1) * BS, cols].astype(jnp.bfloat16)


def backward_kernel(
    heads, cycle, sel_ref, place_ref, info_ref, q_ref, g_ref, k_all, v_all, dq_ref, *rest
):
    own_ref, far_refs = rest[0], rest[1:cycle]
    dk_sum, dv_sum, q_wide, g_wide, k_sel, v_sel, pos = rest[cycle:]
    block = pl.program_id(0)

    @pl.when(block == 0)
    def _():
        q_wide[...] = jnp.zeros_like(q_wide)
        g_wide[...] = jnp.zeros_like(g_wide)
        dk_sum[...] = jnp.zeros_like(dk_sum)
        dv_sum[...] = jnp.zeros_like(dv_sum)

    spread(q_ref, q_wide, heads)
    spread(g_ref, g_wide, heads)
    weights, total = student_weights(
        sel_ref, place_ref, info_ref, q_wide, k_all, v_all, k_sel, v_sel, pos, heads
    )
    weights = weights / total
    weight_grad = dot(v_sel[...], g_wide[...], NT)
    row_dots = jnp.sum(weights * weight_grad, axis=0, keepdims=True)
    score_grad = (weights * (weight_grad - row_dots) * SCALE).astype(jnp.bfloat16)
    query_grad = dot(score_grad, k_sel[...], TN)
    for h in range(heads):
        cols = slice(h * HD, (h + 1) * HD)
        dq_ref[:, cols] = query_grad[h * BS : (h + 1) * BS, cols]
    key_grad = dot(score_grad, q_wide[...])
    value_grad = dot(weights.astype(jnp.bfloat16), g_wide[...])
    for e in range(sel_ref.shape[1]):
        target = pl.ds(pl.multiple_of(place_ref[block, e] * BS, BS), BS)
        dk_sum[target, :] += key_grad[e * BS : (e + 1) * BS, :]
        dv_sum[target, :] += value_grad[e * BS : (e + 1) * BS, :]

    @pl.when(block == pl.num_programs(0) - 1)
    def _():
        rows = own_ref.shape[1]
        own_ref[0] = dk_sum[:rows, :]
        own_ref[1] = dv_sum[:rows, :]
        for d in range(1, cycle):
            far_refs[d - 1][0] = dk_sum[d * rows : (d + 1) * rows, :].astype(jnp.bfloat16)
            far_refs[d - 1][1] = dv_sum[d * rows : (d + 1) * rows, :].astype(jnp.bfloat16)


def student_scratch(heads, keys, wides):
    width = heads * HD
    return [pltpu.VMEM((heads * BS, width), jnp.bfloat16)] * wides + [
        pltpu.VMEM((keys, width), jnp.bfloat16),
        pltpu.VMEM((keys, width), jnp.bfloat16),
        pltpu.VMEM((keys, heads * BS), jnp.int32),
    ]


def student_forward(tables, queries, keys, values):
    rows, width = queries.shape
    tokens = keys.shape[0]
    heads = width // HD
    row_block = pl.BlockSpec((BS, width), lambda b, *_: (b, 0))
    whole = pl.BlockSpec((tokens, width), lambda b, *_: (0, 0))
    return pl.pallas_call(
        functools.partial(forward_kernel, heads),
        grid_spec=pltpu.PrefetchScalarGridSpec(
            num_scalar_prefetch=3,
            grid=(rows // BS,),
            in_specs=[row_block, whole, whole],
            out_specs=row_block,
            scratch_shapes=student_scratch(heads, tables[0].shape[1] * BS, 1),
        ),
        out_shape=jax.ShapeDtypeStruct((rows, width), jnp.bfloat16),
        compiler_params=pltpu.CompilerParams(vmem_limit_bytes=VMEM_LIMIT),
        cost_estimate=pl.CostEstimate(
            flops=16 * rows * tokens * width, bytes_accessed=4 * tokens * width, transcendentals=0
        ),
    )(*tables, queries, keys, values)


def student_backward(tables, queries, grads, keys, values):
    rows, width = queries.shape
    tokens = keys.shape[0]
    cycle = tokens // rows
    heads = width // HD
    row_block = pl.BlockSpec((BS, width), lambda b, *_: (b, 0))
    whole = pl.BlockSpec((tokens, width), lambda b, *_: (0, 0))
    pair = pl.BlockSpec((2, rows, width), lambda b, *_: (0, 0, 0))
    return pl.pallas_call(
        functools.partial(backward_kernel, heads, cycle),
        grid_spec=pltpu.PrefetchScalarGridSpec(
            num_scalar_prefetch=3,
            grid=(rows // BS,),
            in_specs=[row_block, row_block, whole, whole],
            out_specs=[row_block] + [pair] * cycle,
            scratch_shapes=[pltpu.VMEM((tokens, width), jnp.float32)] * 2
            + student_scratch(heads, tables[0].shape[1] * BS, 2),
        ),
        out_shape=[
            jax.ShapeDtypeStruct((rows, width), jnp.float32),
            jax.ShapeDtypeStruct((2, rows, width), jnp.float32),
        ]
        + [jax.ShapeDtypeStruct((2, rows, width), jnp.bfloat16)] * (cycle - 1),
        compiler_params=pltpu.CompilerParams(vmem_limit_bytes=VMEM_LIMIT),
        cost_estimate=pl.CostEstimate(
            flops=32 * rows * tokens * width, bytes_accessed=8 * tokens * width, transcendentals=0
        ),
    )(*tables, queries, grads, keys, values)


def project_kernel(s_attn, t_attn, s_out, t_out, o_ref):
    o_ref[0] = (dot(s_attn[...], s_out[...]) - dot(t_attn[...], t_out[...])).astype(jnp.bfloat16)


def project(s_attn, t_attn, s_out, t_out, groups, s_block=0):
    rows = s_attn.shape[0]
    model = s_out.shape[1]
    tile = model // groups
    return pl.pallas_call(
        project_kernel,
        grid=(groups,),
        in_specs=[
            pl.BlockSpec(s_attn.shape, lambda j: (0, 0)),
            pl.BlockSpec(t_attn.shape, lambda j: (0, 0)),
            pl.BlockSpec((s_attn.shape[1], tile), lambda j: (s_block, j)),
            pl.BlockSpec((t_attn.shape[1], tile), lambda j: (0, j)),
        ],
        out_specs=pl.BlockSpec((1, rows, tile), lambda j: (j, 0, 0)),
        out_shape=jax.ShapeDtypeStruct((groups, rows, tile), jnp.bfloat16),
        compiler_params=pltpu.CompilerParams(vmem_limit_bytes=VMEM_LIMIT),
    )(s_attn, t_attn, s_out, t_out)


def from_earlier(rows, distance):
    route = [(i - distance, i) for i in range(distance, lax.axis_size("blk"))]
    return lax.ppermute(rows, "blk", route)


def on_device(t_query, t_key, t_value, t_out, s_query, s_key, s_value, s_out, segments, selection):
    row_count = t_query.shape[0]
    heads = t_query.shape[1] // HD
    cycle = lax.axis_size("blk")
    split = ("head", "grp")
    groups = lax.axis_size("head") * lax.axis_size("grp")
    my_index = lax.axis_index("blk")
    first_row = my_index * row_count
    shard_blocks = row_count // BS

    count = jnp.sum((segments == 0).astype(jnp.int32)).reshape(1)
    first_count = count
    for distance in range(1, cycle):
        route = [(i, (i + distance) % cycle) for i in range(cycle)]
        first_count = first_count + lax.ppermute(count, "blk", route)
    first_count = first_count[0]
    info = jnp.stack([first_row, first_count]).astype(jnp.int32)

    model_cols = s_out.shape[1] // cycle

    def own_cols(weights):
        return lax.dynamic_slice_in_dim(weights, my_index * model_cols, model_cols, 1)

    s_cols, t_cols = own_cols(s_out), own_cols(t_out)
    s_cols_all = lax.all_gather(s_cols, split, axis=0, tiled=True)
    weights = jnp.concatenate([t_cols, s_cols], axis=0)
    mix = lax.psum(dot(weights, s_cols_all, NT).astype(jnp.bfloat16), "blk")

    if heads % cycle == 0:
        packed = jnp.concatenate(
            [rows.reshape(row_count, heads, HD) for rows in (t_query, t_key, t_value)], axis=2
        ).reshape(row_count, 3 * heads * HD)
        packed = lax.all_to_all(packed, "blk", split_axis=1, concat_axis=0, tiled=True)
        packed, s_key, s_value = lax.optimization_barrier((packed, s_key, s_value))
        whole_heads = teacher(
            packed, packed, packed, heads // cycle, (3, (0, 1, 2)), jnp.int32(0), first_count
        )
        t_attn = lax.all_to_all(whole_heads, "blk", split_axis=0, concat_axis=1, tiled=True)
    else:
        t_attn = teacher(
            t_query,
            lax.all_gather(t_key, "blk", axis=0, tiled=True),
            lax.all_gather(t_value, "blk", axis=0, tiled=True),
            heads,
            (1, (0, 0, 0)),
            first_row,
            first_count,
        )

    key_stack = jnp.concatenate([s_key] + [from_earlier(s_key, d) for d in range(1, cycle)])
    value_stack = jnp.concatenate([s_value] + [from_earlier(s_value, d) for d in range(1, cycle)])
    place = (my_index - selection // shard_blocks) * shard_blocks + selection % shard_blocks
    tables = (selection, place, info)
    s_attn = student_forward(tables, s_query, key_stack, value_stack)

    ratio = t_attn.shape[1] // s_attn.shape[1]
    grad_terms = project(s_attn, t_attn, mix, mix, groups, ratio)
    grads = lax.psum_scatter(grad_terms, split, scatter_dimension=0, tiled=False)
    terms = project(s_attn, t_attn, s_out, t_out, groups)
    terms, grads = lax.optimization_barrier((terms, grads))
    mismatch = lax.psum_scatter(terms, split, scatter_dimension=0, tiled=False)

    grad_query, own, *far = student_backward(
        tables, s_query, grads, key_stack, value_stack
    )
    for distance in range(1, cycle):
        route = [(i, i - distance) for i in range(distance, cycle)]
        own = own + lax.ppermute(far[distance - 1], "blk", route).astype(jnp.float32)
    return (mismatch.astype(jnp.float32), grad_query, own[0], own[1])


def solution(mesh):
    split = ("head", "grp")
    tokens, weights = P("blk", split), P(split, None)
    return jax.shard_map(
        on_device,
        mesh=mesh,
        in_specs=(
            tokens, tokens, tokens, weights, tokens, tokens, tokens, weights, P("blk"),
            P("blk", None),
        ),
        out_specs=(tokens,) * 4,
        check_vma=False,
    )
```

```python
import functools

import jax
import jax.numpy as jnp
from jax import lax
from jax.experimental import pallas as pl
from jax.experimental.pallas import tpu as pltpu
from jax.sharding import PartitionSpec as P

HD = 128
BS = 64
SCALE = HD ** (-0.5)
LOG2E = 1.4426950408889634
MASKED = -1e30
VMEM_LIMIT = 56 * 1024 * 1024

NT = (((1,), (1,)), ((), ()))
TN = (((0,), (0,)), ((), ()))


def dot(a, b, dims=(((1,), (0,)), ((), ()))):
    return lax.dot_general(a, b, dims, preferred_element_type=jnp.float32)


def visible(key_pos, query_pos, first_count):
    low = jnp.where(query_pos < first_count, 0, first_count)
    return (key_pos <= query_pos) & (key_pos >= low)


def teacher_kernel(tile, info_ref, q_ref, k_ref, v_ref, o_ref):
    offset, first_count = info_ref[0], info_ref[1]
    q_tile = q_ref.shape[0]
    q_start = offset + pl.program_id(1) * q_tile
    q_end = q_start + q_tile
    queries = q_ref[...]

    def step(index, carried, masked):
        largest, total, acc = carried
        rows = pl.ds(pl.multiple_of(index * tile, tile), tile)
        scores = dot(k_ref[rows, :], queries, NT)
        if masked:
            key_pos = index * tile + lax.broadcasted_iota(jnp.int32, scores.shape, 0)
            query_pos = q_start + lax.broadcasted_iota(jnp.int32, (1, q_tile), 1)
            scores = jnp.where(visible(key_pos, query_pos, first_count), scores, MASKED)
        new = jnp.maximum(largest, jnp.max(scores, axis=0, keepdims=True))
        weights = jnp.exp2((scores - new) * (SCALE * LOG2E))
        if masked:
            weights = jnp.where(scores > 0.5 * MASKED, weights, 0.0)
        factor = jnp.exp2((largest - new) * (SCALE * LOG2E))
        total = total * factor + jnp.sum(weights, axis=0, keepdims=True)
        acc = acc * factor + dot(v_ref[rows, :], weights.astype(jnp.bfloat16), TN)
        return new, total, acc

    first = jnp.where(q_start >= first_count, first_count // tile, 0)
    last = (q_end + tile - 1) // tile
    straddles = first_count < q_end

    def general(index, carried):
        low, high = index * tile, (index + 1) * tile
        need = (high > q_start) | ((low < first_count) & straddles)
        return lax.cond(
            need,
            lambda c: step(index, c, True),
            lambda c: step(index, c, False),
            carried,
        )

    carried = (
        jnp.full((1, q_tile), MASKED, jnp.float32),
        jnp.zeros((1, q_tile), jnp.float32),
        jnp.zeros((HD, q_tile), jnp.float32),
    )
    _, total, acc = lax.fori_loop(first, last, general, carried)
    o_ref[...] = (acc / total).T.astype(jnp.bfloat16)


def teacher(queries, keys, values, heads, columns, offset, first_count):
    rows, tokens = queries.shape[0], keys.shape[0]
    width = heads * HD
    step, (q_at, k_at, v_at) = columns
    tile = 512
    info = jnp.stack([offset, first_count]).astype(jnp.int32)
    return pl.pallas_call(
        functools.partial(teacher_kernel, tile),
        grid_spec=pltpu.PrefetchScalarGridSpec(
            num_scalar_prefetch=1,
            grid=(heads, rows // tile),
            in_specs=[
                pl.BlockSpec((tile, HD), lambda h, i, s: (i, step * h + q_at)),
                pl.BlockSpec((tokens, HD), lambda h, i, s: (0, step * h + k_at)),
                pl.BlockSpec((tokens, HD), lambda h, i, s: (0, step * h + v_at)),
            ],
            out_specs=pl.BlockSpec((tile, HD), lambda h, i, s: (i, h)),
        ),
        out_shape=jax.ShapeDtypeStruct((rows, width), jnp.bfloat16),
        compiler_params=pltpu.CompilerParams(vmem_limit_bytes=VMEM_LIMIT),
        cost_estimate=pl.CostEstimate(
            flops=2 * rows * tokens * width, bytes_accessed=8 * tokens * width, transcendentals=0
        ),
    )(info, queries, keys, values)


def spread(ref, scratch, heads):
    for h in range(heads):
        cols = slice(h * HD, (h + 1) * HD)
        scratch[h * BS : (h + 1) * BS, cols] = ref[:, cols].astype(scratch.dtype)


def student_weights(sel_ref, place_ref, info_ref, q_wide, k_all, v_all, k_sel, v_sel, pos, heads):
    block = pl.program_id(0)
    count = sel_ref.shape[1]
    offset, first_count = info_ref[0], info_ref[1]
    within = lax.broadcasted_iota(jnp.int32, (BS, 1), 0)
    for e in range(count):
        chosen = sel_ref[block, e]
        source = pl.ds(pl.multiple_of(place_ref[block, e] * BS, BS), BS)
        k_sel[e * BS : (e + 1) * BS, :] = k_all[source, :]
        v_sel[e * BS : (e + 1) * BS, :] = v_all[source, :]
        pos[e * BS : (e + 1) * BS, :] = jnp.broadcast_to(chosen * BS + within, (BS, heads * BS))
    lane = lax.broadcasted_iota(jnp.int32, (1, heads * BS), 1)
    query_pos = offset + block * BS + lax.rem(lane, BS)
    scores = dot(k_sel[...], q_wide[...], NT)
    allowed = visible(pos[...], query_pos, first_count)
    scores = jnp.where(allowed, scores, MASKED)
    largest = jnp.max(scores, axis=0, keepdims=True)
    weights = jnp.exp2((scores - largest) * (SCALE * LOG2E))
    weights = jnp.where(allowed, weights, 0.0)
    return weights, jnp.sum(weights, axis=0, keepdims=True)


def forward_kernel(heads, sel_ref, place_ref, info_ref, q_ref, k_all, v_all, o_ref, q_wide, k_sel, v_sel, pos):
    @pl.when(pl.program_id(0) == 0)
    def _():
        q_wide[...] = jnp.zeros_like(q_wide)

    spread(q_ref, q_wide, heads)
    weights, total = student_weights(
        sel_ref, place_ref, info_ref, q_wide, k_all, v_all, k_sel, v_sel, pos, heads
    )
    weights = (weights / total).astype(jnp.bfloat16)
    blended = dot(weights, v_sel[...], TN)
    for h in range(heads):
        cols = slice(h * HD, (h + 1) * HD)
        o_ref[:, cols] = blended[h * BS : (h + 1) * BS, cols].astype(jnp.bfloat16)


def backward_kernel(
    heads, cycle, sel_ref, place_ref, info_ref, q_ref, g_ref, k_all, v_all, dq_ref, *rest
):
    own_ref, far_refs = rest[0], rest[1:cycle]
    dk_sum, dv_sum, q_wide, g_wide, k_sel, v_sel, pos = rest[cycle:]
    block = pl.program_id(0)

    @pl.when(block == 0)
    def _():
        q_wide[...] = jnp.zeros_like(q_wide)
        g_wide[...] = jnp.zeros_like(g_wide)
        dk_sum[...] = jnp.zeros_like(dk_sum)
        dv_sum[...] = jnp.zeros_like(dv_sum)

    spread(q_ref, q_wide, heads)
    spread(g_ref, g_wide, heads)
    weights, total = student_weights(
        sel_ref, place_ref, info_ref, q_wide, k_all, v_all, k_sel, v_sel, pos, heads
    )
    weights = weights / total
    weight_grad = dot(v_sel[...], g_wide[...], NT)
    row_dots = jnp.sum(weights * weight_grad, axis=0, keepdims=True)
    score_grad = (weights * (weight_grad - row_dots) * SCALE).astype(jnp.bfloat16)
    query_grad = dot(score_grad, k_sel[...], TN)
    for h in range(heads):
        cols = slice(h * HD, (h + 1) * HD)
        dq_ref[:, cols] = query_grad[h * BS : (h + 1) * BS, cols]
    key_grad = dot(score_grad, q_wide[...])
    value_grad = dot(weights.astype(jnp.bfloat16), g_wide[...])
    for e in range(sel_ref.shape[1]):
        target = pl.ds(pl.multiple_of(place_ref[block, e] * BS, BS), BS)
        dk_sum[target, :] += key_grad[e * BS : (e + 1) * BS, :]
        dv_sum[target, :] += value_grad[e * BS : (e + 1) * BS, :]

    @pl.when(block == pl.num_programs(0) - 1)
    def _():
        rows = own_ref.shape[1]
        own_ref[0] = dk_sum[:rows, :]
        own_ref[1] = dv_sum[:rows, :]
        for d in range(1, cycle):
            far_refs[d - 1][0] = dk_sum[d * rows : (d + 1) * rows, :].astype(jnp.bfloat16)
            far_refs[d - 1][1] = dv_sum[d * rows : (d + 1) * rows, :].astype(jnp.bfloat16)


def student_scratch(heads, keys, wides):
    width = heads * HD
    return [pltpu.VMEM((heads * BS, width), jnp.bfloat16)] * wides + [
        pltpu.VMEM((keys, width), jnp.bfloat16),
        pltpu.VMEM((keys, width), jnp.bfloat16),
        pltpu.VMEM((keys, heads * BS), jnp.int32),
    ]


def student_forward(tables, queries, keys, values):
    rows, width = queries.shape
    tokens = keys.shape[0]
    heads = width // HD
    row_block = pl.BlockSpec((BS, width), lambda b, *_: (b, 0))
    whole = pl.BlockSpec((tokens, width), lambda b, *_: (0, 0))
    return pl.pallas_call(
        functools.partial(forward_kernel, heads),
        grid_spec=pltpu.PrefetchScalarGridSpec(
            num_scalar_prefetch=3,
            grid=(rows // BS,),
            in_specs=[row_block, whole, whole],
            out_specs=row_block,
            scratch_shapes=student_scratch(heads, tables[0].shape[1] * BS, 1),
        ),
        out_shape=jax.ShapeDtypeStruct((rows, width), jnp.bfloat16),
        compiler_params=pltpu.CompilerParams(vmem_limit_bytes=VMEM_LIMIT),
        cost_estimate=pl.CostEstimate(
            flops=16 * rows * tokens * width, bytes_accessed=4 * tokens * width, transcendentals=0
        ),
    )(*tables, queries, keys, values)


def student_backward(tables, queries, grads, keys, values):
    rows, width = queries.shape
    tokens = keys.shape[0]
    cycle = tokens // rows
    heads = width // HD
    row_block = pl.BlockSpec((BS, width), lambda b, *_: (b, 0))
    whole = pl.BlockSpec((tokens, width), lambda b, *_: (0, 0))
    pair = pl.BlockSpec((2, rows, width), lambda b, *_: (0, 0, 0))
    return pl.pallas_call(
        functools.partial(backward_kernel, heads, cycle),
        grid_spec=pltpu.PrefetchScalarGridSpec(
            num_scalar_prefetch=3,
            grid=(rows // BS,),
            in_specs=[row_block, row_block, whole, whole],
            out_specs=[row_block] + [pair] * cycle,
            scratch_shapes=[pltpu.VMEM((tokens, width), jnp.float32)] * 2
            + student_scratch(heads, tables[0].shape[1] * BS, 2),
        ),
        out_shape=[
            jax.ShapeDtypeStruct((rows, width), jnp.float32),
            jax.ShapeDtypeStruct((2, rows, width), jnp.float32),
        ]
        + [jax.ShapeDtypeStruct((2, rows, width), jnp.bfloat16)] * (cycle - 1),
        compiler_params=pltpu.CompilerParams(vmem_limit_bytes=VMEM_LIMIT),
        cost_estimate=pl.CostEstimate(
            flops=32 * rows * tokens * width, bytes_accessed=8 * tokens * width, transcendentals=0
        ),
    )(*tables, queries, grads, keys, values)


def project_kernel(s_attn, t_attn, s_out, t_out, o_ref):
    o_ref[0] = (dot(s_attn[...], s_out[...]) - dot(t_attn[...], t_out[...])).astype(jnp.bfloat16)


def project(s_attn, t_attn, s_out, t_out, groups):
    rows = s_attn.shape[0]
    model = s_out.shape[1]
    tile = model // groups
    return pl.pallas_call(
        project_kernel,
        grid=(groups,),
        in_specs=[
            pl.BlockSpec(s_attn.shape, lambda j: (0, 0)),
            pl.BlockSpec(t_attn.shape, lambda j: (0, 0)),
            pl.BlockSpec((s_attn.shape[1], tile), lambda j: (0, j)),
            pl.BlockSpec((t_attn.shape[1], tile), lambda j: (0, j)),
        ],
        out_specs=pl.BlockSpec((1, rows, tile), lambda j: (j, 0, 0)),
        out_shape=jax.ShapeDtypeStruct((groups, rows, tile), jnp.bfloat16),
        compiler_params=pltpu.CompilerParams(vmem_limit_bytes=VMEM_LIMIT),
    )(s_attn, t_attn, s_out, t_out)


def mixed_kernel(s_attn, t_attn, s_mix, t_mix, o_ref):
    part = dot(s_attn[...], s_mix[...], NT) - dot(t_attn[...], t_mix[...], NT)
    o_ref[0] = part.astype(jnp.bfloat16)


def project_mixed(s_attn, t_attn, mix, groups, s_block):
    rows = s_attn.shape[0]
    tile = mix.shape[0] // groups
    return pl.pallas_call(
        mixed_kernel,
        grid=(groups,),
        in_specs=[
            pl.BlockSpec(s_attn.shape, lambda j: (0, 0)),
            pl.BlockSpec(t_attn.shape, lambda j: (0, 0)),
            pl.BlockSpec((tile, s_attn.shape[1]), lambda j: (j, s_block)),
            pl.BlockSpec((tile, t_attn.shape[1]), lambda j: (j, 0)),
        ],
        out_specs=pl.BlockSpec((1, rows, tile), lambda j: (j, 0, 0)),
        out_shape=jax.ShapeDtypeStruct((groups, rows, tile), jnp.bfloat16),
        compiler_params=pltpu.CompilerParams(vmem_limit_bytes=VMEM_LIMIT),
    )(s_attn, t_attn, mix, mix)


def from_earlier(rows, distance):
    route = [(i - distance, i) for i in range(distance, lax.axis_size("blk"))]
    return lax.ppermute(rows, "blk", route)


def on_device(t_query, t_key, t_value, t_out, s_query, s_key, s_value, s_out, segments, selection):
    row_count = t_query.shape[0]
    heads = t_query.shape[1] // HD
    cycle = lax.axis_size("blk")
    split = ("head", "grp")
    groups = lax.axis_size("head") * lax.axis_size("grp")
    my_index = lax.axis_index("blk")
    first_row = my_index * row_count
    shard_blocks = row_count // BS

    count = jnp.sum((segments == 0).astype(jnp.int32)).reshape(1)
    first_count = count
    for distance in range(1, cycle):
        route = [(i, (i + distance) % cycle) for i in range(cycle)]
        first_count = first_count + lax.ppermute(count, "blk", route)
    first_count = first_count[0]
    info = jnp.stack([first_row, first_count]).astype(jnp.int32)

    model_cols = s_out.shape[1] // cycle

    def own_cols(weights):
        return lax.dynamic_slice_in_dim(weights, my_index * model_cols, model_cols, 1)

    s_cols, t_cols = own_cols(s_out), own_cols(t_out)
    s_cols_all = lax.all_gather(s_cols, split, axis=0, tiled=True)
    weights = jnp.concatenate([t_cols, s_cols], axis=0)
    if heads % cycle == 0:
        packed = jnp.concatenate(
            [rows.reshape(row_count, heads, HD) for rows in (t_query, t_key, t_value)], axis=2
        ).reshape(row_count, 3 * heads * HD)
        packed = lax.all_to_all(packed, "blk", split_axis=1, concat_axis=0, tiled=True)
        packed, s_key, s_value, s_cols_all = lax.optimization_barrier(
            (packed, s_key, s_value, s_cols_all)
        )
        whole_heads = teacher(
            packed, packed, packed, heads // cycle, (3, (0, 1, 2)), jnp.int32(0), first_count
        )
        t_attn = lax.all_to_all(whole_heads, "blk", split_axis=0, concat_axis=1, tiled=True)
    else:
        t_attn = teacher(
            t_query,
            lax.all_gather(t_key, "blk", axis=0, tiled=True),
            lax.all_gather(t_value, "blk", axis=0, tiled=True),
            heads,
            (1, (0, 0, 0)),
            first_row,
            first_count,
        )

    mix = dot(s_cols_all, weights, NT).astype(jnp.bfloat16)
    mix = lax.psum_scatter(mix, "blk", scatter_dimension=0, tiled=True)
    mix = lax.all_gather(mix, "blk", axis=0, tiled=True)

    key_stack = jnp.concatenate([s_key] + [from_earlier(s_key, d) for d in range(1, cycle)])
    value_stack = jnp.concatenate([s_value] + [from_earlier(s_value, d) for d in range(1, cycle)])
    place = (my_index - selection // shard_blocks) * shard_blocks + selection % shard_blocks
    tables = (selection, place, info)
    s_attn = student_forward(tables, s_query, key_stack, value_stack)

    ratio = t_attn.shape[1] // s_attn.shape[1]
    grad_terms = project_mixed(s_attn, t_attn, mix, groups, ratio)
    grads = lax.psum_scatter(grad_terms, split, scatter_dimension=0, tiled=False)
    terms = project(s_attn, t_attn, s_out, t_out, groups)
    terms, grads = lax.optimization_barrier((terms, grads))
    mismatch = lax.psum_scatter(terms, split, scatter_dimension=0, tiled=False)

    grad_query, own, *far = student_backward(
        tables, s_query, grads, key_stack, value_stack
    )
    for distance in range(1, cycle):
        route = [(i, i - distance) for i in range(distance, cycle)]
        own = own + lax.ppermute(far[distance - 1], "blk", route).astype(jnp.float32)
    return (mismatch.astype(jnp.float32), grad_query, own[0], own[1])


def solution(mesh):
    split = ("head", "grp")
    tokens, weights = P("blk", split), P(split, None)
    return jax.shard_map(
        on_device,
        mesh=mesh,
        in_specs=(
            tokens, tokens, tokens, weights, tokens, tokens, tokens, weights, P("blk"),
            P("blk", None),
        ),
        out_specs=(tokens,) * 4,
        check_vma=False,
    )
```
